128 devices in a mesh: lat: 16 (over y, x), lev: 8 (over z, core).
Axes of the slice: x: 4, y: 4, z: 4, core: 2. Of those that a mesh axis runs over, the one named last changes fastest.
Arguments:
- fourier: bfloat16 [2560, 96, 1024], P('lat', 'lev'), may hold values from -6 to 6
- table: int32 [512], replicated, may hold values from 0 to 511, each once
- legendre: bfloat16 [512, 2, 513, 1280], P(('lat', 'lev')), may hold values from -0.15625 to 0.15625
Outputs:
- spectral: bfloat16 [512, 2, 96, 513], P(('lat', 'lev'))
The draws below stay inside these ranges and needn't reach their ends.
Inputs may be any that keep to these rules, and one draw needn't show every extreme that they name: `table`: every pair index appears exactly once.
All inputs are finite; a program needn't handle non-finite values.
Results may differ from the reference program's by a relative error of at most 0.0051.
Values may be sent and summed in bfloat16 or wider, within the bound.
A program may use at most 128 MiB of HBM per device.

```python
import jax
import jax.numpy as jnp
from jax import lax

NLAT = 2560
JH = 1280
PAIRS = 512
M = 1024
R = 513
C = 96


def level_of(rng, extent, pieces, least, top_value):
    def one(dim, blocks):
        draws = jax.random.uniform(jax.random.fold_in(jax.random.fold_in(rng, 6), dim), (blocks,), jnp.float32, least / len(pieces), top_value / len(pieces))
        return jnp.repeat(jnp.exp(draws), extent[dim] // blocks).reshape((-1,) + (1,) * (len(extent) - dim - 1))

    factor_of = one(*pieces[0])
    for cut in pieces[1:]:
        factor_of = factor_of * one(*cut)
    return factor_of


def normal_values(own_key, dims, deviation, limit, shards=(), held_as=jnp.bfloat16):
    drawn = jax.random.normal(own_key, dims, jnp.float32) * deviation
    if len(shards) > 0:
        drawn = level_of(own_key, dims, shards, -0.22, 0.18) * drawn
    return jnp.clip(drawn, min=-limit, max=limit).astype(held_as)


def setup_inputs(seed: int = 0) -> dict:
    key_list = jax.random.split(jax.random.key(seed), 4)
    return {
        "fourier": normal_values(key_list[0], (NLAT, C, M), 1.0, 6.0, ((0, 16), (1, 8))),
        "table": jax.random.permutation(key_list[1], PAIRS).astype(jnp.int32),
        "legendre": normal_values(key_list[2], (PAIRS, 2, R, JH), JH ** -0.5, 0.15625, ((0, 128),)),
    }


def transform_pair(combined, pair_index, tables):
    columns = jnp.stack([pair_index, M - 1 - pair_index]).astype(jnp.int32)
    selected = jnp.take(combined, columns, axis=3).astype(jnp.float32)
    products = jnp.einsum("erj,ejcw->ewcr", tables.astype(jnp.float32), selected)
    parity = jnp.arange(2).astype(jnp.int32)
    row_counts = (M - pair_index - parity + 1) // 2
    first_member = jnp.arange(R).astype(jnp.int32)[None, :] < row_counts[:, None]
    return jnp.where(first_member[:, None, :], products[:, 0], products[:, 1]).astype(jnp.bfloat16)


def reference(fourier, table, legendre):
    northern = fourier[:JH].astype(jnp.float32)
    southern = fourier[JH:].astype(jnp.float32)
    combined = jnp.stack([(northern + southern).astype(jnp.bfloat16), (northern - southern).astype(jnp.bfloat16)])

    def per_slot(pair_entry):
        return transform_pair(combined, pair_entry[0], pair_entry[1])

    return lax.map(per_slot, (table, legendre))
```

```python
import functools

import jax
import jax.numpy as jnp
from jax import lax
from jax.experimental import pallas as pl
from jax.experimental.pallas import tpu as pltpu
from jax.sharding import PartitionSpec as P

MESH = pl.DeviceIdType.MESH
F32, BF16 = jnp.float32, jnp.bfloat16
SIDE = 4
LEVS = 8
DEVICES = 128
GROUPS = 4
RUN = DEVICES // GROUPS
ROWS = 8
ORDER = (2 | 8 | 32, 8, 16, 32, 64, 1, 4)
NT = (((1,), (1,)), ((), ()))


def hop(k):
    bits = 0
    for place, mask in enumerate(ORDER):
        bits = bits ^ (((k >> place) & 1) * mask)
    return bits & 3, (bits >> 2) & 3, (bits >> 4) & 3, (bits >> 6) & 1


def where_am_i():
    lat, lev = lax.axis_index("lat"), lax.axis_index("lev")
    return lat, lev, lat % SIDE, lat // SIDE


def target(k):
    lat, lev, x, y = where_am_i()
    dx, dy, dz, dc = hop(k)
    z, core = lev // 2, lev % 2
    return (y + dy) % SIDE * SIDE + (x + dx) % SIDE, (z + dz) % SIDE * 2 + (core + dc) % 2


def fused(
    table, fourier, legendre, spectral,
    rows_in, picks, outgoing, arrived, raw_tables, tables, spread, lanes, parts, totals,
    rows_sem, table_sem, send_sem, recv_sem, own_sem, plane_sem, all_sem,
):
    channels, lat_rows, width = fourier.shape
    slot_count, degree_rows = legendre.shape[0], legendre.shape[1]
    lat, lev, x, y = where_am_i()
    me = lat * LEVS + lev
    tail = lat_rows - 128
    fold = 128 // tail

    barrier = pltpu.get_barrier_semaphore()
    x_line = [(y * SIDE + (x + i) % SIDE, lev) for i in range(1, SIDE)]
    y_line = [((y + i) % SIDE * SIDE + x, lev) for i in range(1, SIDE)]
    z_line = [(lat, (lev + i) % LEVS) for i in range(1, LEVS)]
    for peer in x_line + y_line + z_line:
        pl.semaphore_signal(barrier, inc=1, device_id=peer, device_id_type=MESH)

    for c in range(channels):
        pltpu.make_async_copy(
            fourier.at[c, pl.ds(0, 128)], rows_in.at[pl.ds(c * 128, 128)], rows_sem
        ).start()
        pltpu.make_async_copy(
            fourier.at[c, pl.ds(128, tail)], rows_in.at[pl.ds(channels * 128 + c * tail, tail)], rows_sem
        ).start()
    for s in range(slot_count):
        pltpu.make_async_copy(legendre.at[s], raw_tables.at[s], table_sem.at[s]).start()

    sub = lax.broadcasted_iota(jnp.int32, (ROWS, width), 0)
    lane = lax.broadcasted_iota(jnp.int32, (ROWS, width), 1)

    def pick(k, carry):
        to_lat, to_lev = target(k)
        first = (to_lat * LEVS + to_lev) * slot_count
        pair = jnp.full((ROWS, width), table[first], jnp.int32)
        for s in range(1, slot_count):
            pair = jnp.where(sub // 2 == s, table[first + s], pair)
        column = jnp.where(sub % 2 == 0, pair, width - 1 - pair)
        picks[k] = jnp.where(lane == column, 1.0, 0.0).astype(BF16)
        return carry

    lax.fori_loop(0, DEVICES, pick, 0)
    pltpu.make_async_copy(rows_in, rows_in, rows_sem).wait()

    step = 384

    def gather(m):
        chosen = picks[pl.ds(m * RUN, RUN)].reshape(RUN * ROWS, width)

        def some(n, carry):
            at = pl.multiple_of(n * step, 128)
            got = lax.dot_general(
                chosen, rows_in[pl.ds(at, step), :], NT, preferred_element_type=F32
            )
            outgoing[pl.ds(m * RUN, RUN), :, pl.ds(at, step)] = got.astype(BF16).reshape(RUN, ROWS, step)
            return carry

        lax.fori_loop(0, channels * lat_rows // step, some, 0)

    gather(0)
    pl.semaphore_wait(barrier, len(x_line) + len(y_line) + len(z_line))
    for peer in y_line:
        pl.semaphore_signal(plane_sem, inc=1, device_id=peer, device_id_type=MESH)
    gather(1)
    pl.semaphore_wait(plane_sem, len(y_line))
    for peer in z_line:
        pl.semaphore_signal(all_sem, inc=1, device_id=peer, device_id_type=MESH)
    gather(2)
    gather(3)
    own = pltpu.make_async_copy(outgoing.at[0], arrived.at[me], own_sem)
    own.start()
    pl.semaphore_wait(all_sem, len(z_line))

    for m in range(GROUPS):
        def send(k, carry):
            pltpu.make_async_remote_copy(
                src_ref=outgoing.at[k],
                dst_ref=arrived.at[me],
                send_sem=send_sem,
                recv_sem=recv_sem.at[m],
                device_id=target(k),
                device_id_type=MESH,
            ).start()
            return carry

        lax.fori_loop(max(1, m * RUN), (m + 1) * RUN, send, 0)

    ri = lax.broadcasted_iota(jnp.int32, (256, 256), 0)
    ci = lax.broadcasted_iota(jnp.int32, (256, 256), 1)
    spread[...] = jnp.where(ci == ri % 128 * 2 + ri // 128, 1.0, 0.0).astype(BF16)
    source = jnp.where(ci < 128, ci, 128 + ci % tail)
    for q in range(fold):
        lanes[q] = jnp.where(ri == source + q * tail, 1.0, 0.0).astype(BF16)
    r_last = lax.broadcasted_iota(jnp.int32, (32, 256), 0)
    c_last = lax.broadcasted_iota(jnp.int32, (32, 256), 1)
    last = jnp.where((r_last % 16 == 0) & (c_last == 254 + r_last // 16), 1.0, 0.0).astype(BF16)

    def relay(s, start, chooser, at, count):
        raw = raw_tables[s, pl.ds(start, 128)].reshape(256, raw_tables.shape[3])
        apart = jnp.dot(chooser, raw, preferred_element_type=F32).astype(BF16)
        for a in range(LEVS):
            low = lat_rows * a // 128 * 128
            laid = jnp.dot(apart[:, low : low + 256], lanes[a % fold], preferred_element_type=F32).astype(BF16)
            g = a // SIDE * 2 + a % 2
            half = a % SIDE // 2
            for e in range(2):
                tables[g, s, e, pl.ds(at, count), half * 256 : half * 256 + 256] = laid[e * count : (e + 1) * count]

    for s in range(slot_count):
        pltpu.make_async_copy(legendre.at[s], raw_tables.at[s], table_sem.at[s]).wait()

        def block(j, carry):
            at = pl.multiple_of(j * 128, 128)
            relay(s, at, spread[...], at, 128)
            return carry

        lax.fori_loop(0, degree_rows // 128, block, 0)
        relay(s, degree_rows - 128, last, degree_rows - 1, 16)

    own.wait()
    lane8 = lax.broadcasted_iota(jnp.int32, (ROWS, 128), 1)
    for m in range(GROUPS):
        count = RUN - 1 if m == 0 else RUN
        some = arrived.at[pl.ds(0, count)]
        pltpu.make_async_copy(some, some, recv_sem.at[m]).wait()
        from_x, from_y = (x + m) % 2, (y + m // 2) % 2
        g = from_y * 2 + from_x
        for half in range(2):
            north = from_y * SIDE + from_x + 2 * half

            def fold_in(b, carry):
                upper = arrived[north * LEVS + b].astype(F32)
                lower = arrived[(north + 8) * LEVS + b].astype(F32)
                for e, both in enumerate((upper + lower, upper - lower)):
                    for c in range(channels):
                        at = pl.ds(pl.multiple_of((b * channels + c) * ROWS, ROWS), ROWS)
                        parts[half * 2, e, at, :] = both[:, c * 128 : c * 128 + 128]
                        rest = channels * 128 + c // fold * 128
                        parts[half * 2 + 1, e, at, :] = jnp.where(
                            lane8 // tail == c % fold, both[:, rest : rest + 128], 0.0
                        )
                return carry

            lax.fori_loop(0, LEVS, fold_in, 0)

        def multiply(n, carry):
            s, e = n // 2, n % 2
            left = jnp.concatenate(
                [
                    jnp.concatenate(
                        [
                            parts[i, e, pl.ds(2 * s + w, LEVS * channels, stride=ROWS), :].astype(BF16)
                            for i in range(4)
                        ],
                        axis=1,
                    )
                    for w in range(2)
                ],
                axis=0,
            )
            product = lax.dot_general(left, tables[g, s, e], NT, preferred_element_type=F32)
            if m == 0:
                totals[s, e] = product
            elif m < GROUPS - 1:
                totals[s, e] += product
            else:
                product = totals[s, e] + product
                limit = (width - table[me * slot_count + s] - e + 1) // 2
                degree = lax.broadcasted_iota(jnp.int32, (LEVS * channels, product.shape[1]), 1)
                chosen = jnp.where(degree < limit, product[: LEVS * channels], product[LEVS * channels :])
                spectral[s, e] = chosen[:, :degree_rows].astype(BF16)
            return carry

        lax.fori_loop(0, 2 * slot_count, multiply, 0)

    sent = outgoing.at[pl.ds(0, DEVICES - 1)]
    pltpu.make_async_copy(sent, sent, send_sem).wait()


def on_device(fourier, table, legendre):
    lat_rows, channels, width = fourier.shape
    slot_count, _, degree_rows, half_lats = legendre.shape
    padded = (degree_rows + 15) // 16 * 16
    return pl.pallas_call(
        fused,
        out_shape=jax.ShapeDtypeStruct((slot_count, 2, LEVS * channels, degree_rows), BF16),
        in_specs=[
            pl.BlockSpec(memory_space=pltpu.SMEM),
            pl.BlockSpec(memory_space=pltpu.HBM),
            pl.BlockSpec(memory_space=pltpu.HBM),
        ],
        out_specs=pl.BlockSpec(memory_space=pltpu.VMEM),
        scratch_shapes=[
            pltpu.VMEM((channels * lat_rows, width), BF16),
            pltpu.VMEM((DEVICES, ROWS, width), BF16),
            pltpu.VMEM((DEVICES, ROWS, channels * lat_rows), BF16),
            pltpu.VMEM((DEVICES, ROWS, channels * lat_rows), BF16),
            pltpu.VMEM((slot_count, degree_rows, 2, half_lats), BF16),
            pltpu.VMEM((GROUPS, slot_count, 2, padded, 512), BF16),
            pltpu.VMEM((256, 256), BF16),
            pltpu.VMEM((4, 256, 256), BF16),
            pltpu.VMEM((4, 2, LEVS * channels * ROWS, 128), F32),
            pltpu.VMEM((slot_count, 2, 2 * LEVS * channels, padded), F32),
            pltpu.SemaphoreType.DMA,
            pltpu.SemaphoreType.DMA((slot_count,)),
            pltpu.SemaphoreType.DMA,
            pltpu.SemaphoreType.DMA((GROUPS,)),
            pltpu.SemaphoreType.DMA,
            pltpu.SemaphoreType.REGULAR,
            pltpu.SemaphoreType.REGULAR,
        ],
        compiler_params=pltpu.CompilerParams(
            collective_id=0, has_side_effects=True, vmem_limit_bytes=63 << 20
        ),
    )(table, fourier.transpose(1, 0, 2), legendre.transpose(0, 2, 1, 3))


def solution(mesh):
    in_specs = (P("lat", "lev", None), P(), P(("lat", "lev"), None, None, None))
    out_specs = P(("lat", "lev"), None, None, None)
    return jax.shard_map(
        on_device, mesh=mesh, in_specs=in_specs, out_specs=out_specs, check_vma=False
    )
```

```python
import functools

import jax
import jax.numpy as jnp
from jax import lax
from jax.experimental import pallas as pl
from jax.experimental.pallas import tpu as pltpu
from jax.sharding import PartitionSpec as P

MESH = pl.DeviceIdType.MESH
F32, BF16 = jnp.float32, jnp.bfloat16
SIDE = 4
LEVS = 8
DEVICES = 128
GROUPS = 4
RUN = DEVICES // GROUPS
ROWS = 8
ORDER = (2 | 8 | 32, 32, 8, 16, 64)
NT = (((1,), (1,)), ((), ()))


def hop(i):
    bits = 0
    for place, mask in enumerate(ORDER):
        bits ^= (i >> place & 1) * mask
    return bits & 2, bits >> 2 & 2, bits >> 4 & 3, bits >> 6


def targets(m):
    lat, lev = lax.axis_index("lat"), lax.axis_index("lev")
    x, y, z, core = lat % SIDE + m % 2, lat // SIDE + m // 2, lev // 2, lev % 2
    xs = {d: (x + d) % SIDE for d in (0, 2)}
    ys = {d: (y + d) % SIDE * SIDE for d in (0, 2)}
    zs = {d: (z + d) % SIDE * 2 for d in range(SIDE)}
    lats = {(dx, dy): ys[dy] + xs[dx] for dx in xs for dy in ys}
    levs = {(dz, dc): zs[dz] + (core + dc) % 2 for dz in zs for dc in range(2)}
    hops = [hop(i) for i in range(RUN)]
    return [(lats[dx, dy], levs[dz, dc]) for dx, dy, dz, dc in hops]


def fused(
    table, fourier, legendre, spectral,
    rows_in, picks, outgoing, arrived, raw_tables, tables, spread, lanes, last_rows, parts, totals, last_totals,
    rows_sem, table_sem, send_sem, recv_sem, own_sem, all_sem,
):
    channels, lat_rows, width = fourier.shape
    slot_count, degree_rows = legendre.shape[0], legendre.shape[1]
    lat, lev = lax.axis_index("lat"), lax.axis_index("lev")
    x, y = lat % SIDE, lat // SIDE
    me = lat * LEVS + lev
    tail = lat_rows - 128
    fold = 128 // tail

    near = targets(0)[1:]
    links = [targets(m)[0] for m in range(1, GROUPS)]
    back = [((y - m // 2) % SIDE * SIDE + (x - m % 2) % SIDE, lev) for m in range(1, GROUPS)]
    barrier = pltpu.get_barrier_semaphore()
    for peer in near + links:
        pl.semaphore_signal(barrier, inc=1, device_id=peer, device_id_type=MESH)

    step = 384
    pieces = channels * lat_rows // step

    def piece(i):
        return rows_in.at[pl.ds(pl.multiple_of(i * step, 128), step)]

    for c in range(channels):
        pltpu.make_async_copy(
            fourier.at[c, pl.ds(0, 128)], rows_in.at[pl.ds(c * 128, 128)], rows_sem.at[c * 128 // step]
        ).start()
    for c in range(channels):
        pltpu.make_async_copy(
            fourier.at[c, pl.ds(128, tail)],
            rows_in.at[pl.ds(channels * 128 + c * tail, tail)],
            rows_sem.at[pieces - 1],
        ).start()
    for s in range(slot_count):
        pltpu.make_async_copy(legendre.at[s], raw_tables.at[s], table_sem.at[s]).start()

    sub = lax.broadcasted_iota(jnp.int32, (ROWS, 128), 0)
    lane = lax.broadcasted_iota(jnp.int32, (ROWS, 128), 1)

    def choose(m):
        for i, (to_lat, to_lev) in enumerate(targets(m)):
            first = (to_lat * LEVS + to_lev) * slot_count
            pair = jnp.full((ROWS, 128), table[first], jnp.int32)
            for s in range(1, slot_count):
                pair = jnp.where(sub // 2 == s, table[first + s], pair)
            column = jnp.where(sub % 2 == 0, pair, width - 1 - pair) - lane
            for t in range(width // 128):
                picks[i, :, t * 128 : t * 128 + 128] = jnp.where(column == t * 128, 1.0, 0.0).astype(BF16)

    def gather(m):
        choose(m)

        def some(i, carry):
            if m == 0:
                pltpu.make_async_copy(piece(i), piece(i), rows_sem.at[i]).wait()
            got = lax.dot_general(
                picks[...].reshape(RUN * ROWS, width), piece(i)[...], NT, preferred_element_type=F32
            )
            at = pl.ds(pl.multiple_of(i * step, 128), step)
            outgoing[m * RUN : (m + 1) * RUN, :, at] = got.astype(BF16).reshape(RUN, ROWS, step)
            return carry

        lax.fori_loop(0, pieces, some, 0)

    def send(m):
        for i, peer in enumerate(targets(m)):
            if m == 0 and i == 0:
                continue
            pltpu.make_async_remote_copy(
                src_ref=outgoing.at[m * RUN + i],
                dst_ref=arrived.at[me],
                send_sem=send_sem,
                recv_sem=recv_sem.at[m],
                device_id=peer,
                device_id_type=MESH,
            ).start()

    gather(0)
    pl.semaphore_wait(barrier, len(near) + len(links))
    for peer in back:
        pl.semaphore_signal(all_sem, inc=1, device_id=peer, device_id_type=MESH)
    send(0)
    own = pltpu.make_async_copy(outgoing.at[0], arrived.at[me], own_sem)
    own.start()
    gather(1)
    pl.semaphore_wait(all_sem, len(links))
    gather(2)
    send(1)
    gather(3)
    send(2)

    ri = lax.broadcasted_iota(jnp.int32, (256, 256), 0)
    ci = lax.broadcasted_iota(jnp.int32, (256, 256), 1)
    spread[...] = jnp.where(ci == ri % 128 * 2 + ri // 128, 1.0, 0.0).astype(BF16)
    source = jnp.where(ri < 128, ri, 128 + ri % tail)
    for q in range(fold):
        lanes[q] = jnp.where(ci == source + q * tail, 1.0, 0.0).astype(BF16)
    r_last = lax.broadcasted_iota(jnp.int32, (16, 256), 0)
    c_last = lax.broadcasted_iota(jnp.int32, (16, 256), 1)
    last = jnp.where(c_last == 254 + r_last // 8, 1.0, 0.0).astype(BF16)

    def relay(s, start, chooser):
        raw = raw_tables[s, pl.ds(start, 128)].reshape(256, raw_tables.shape[3])
        apart = jnp.dot(chooser, raw, preferred_element_type=F32).astype(BF16)
        for a in range(LEVS):
            low = lat_rows * a // 128 * 128
            yield a // SIDE * 2 + a % 2, a % SIDE // 2 * 256, apart[:, low : low + 256], lanes[a % fold]

    for s in range(slot_count):
        pltpu.make_async_copy(legendre.at[s], raw_tables.at[s], table_sem.at[s]).wait()

        def block(j, carry):
            at = pl.multiple_of(j * 128, 128)
            for g, place, apart, layout in relay(s, at, spread[...]):
                laid = lax.dot_general(layout, apart, NT, preferred_element_type=F32).astype(BF16)
                for e in range(2):
                    tables[g, s, e, place : place + 256, pl.ds(at, 128)] = laid[:, e * 128 : e * 128 + 128]
            return carry

        lax.fori_loop(0, degree_rows // 128, block, 0)
        for g, place, apart, layout in relay(s, degree_rows - 128, last):
            laid = lax.dot_general(apart, layout, NT, preferred_element_type=F32)
            for e in range(2):
                last_rows[g, s, e, :, place : place + 256] = laid[e * 8 : e * 8 + 8]
        if s == 0:
            send(3)

    own.wait()
    lane8 = lax.broadcasted_iota(jnp.int32, (ROWS, 128), 1)
    for m in range(GROUPS):
        count = DEVICES // GROUPS - (1 if m == 0 else 0)
        some = arrived.at[pl.ds(0, count)]
        pltpu.make_async_copy(some, some, recv_sem.at[m]).wait()
        from_x, from_y = (x + m) % 2, (y + m // 2) % 2
        g = from_y * 2 + from_x
        for half in range(2):
            north = from_y * SIDE + from_x + 2 * half

            def fold_in(b, carry):
                upper = arrived[north * LEVS + b].astype(F32)
                lower = arrived[(north + 8) * LEVS + b].astype(F32)
                for e, both in enumerate((upper + lower, upper - lower)):
                    for c in range(channels):
                        at = pl.ds(pl.multiple_of((b * channels + c) * ROWS, ROWS), ROWS)
                        parts[half * 2, e, at, :] = both[:, c * 128 : c * 128 + 128]
                        rest = channels * 128 + c // fold * 128
                        parts[half * 2 + 1, e, at, :] = jnp.where(
                            lane8 // tail == c % fold, both[:, rest : rest + 128], 0.0
                        )
                return carry

            lax.fori_loop(0, LEVS, fold_in, 0)

        def multiply(n, carry):
            s, e = n // 2, n % 2
            sides = [
                [parts[i, e, pl.ds(2 * s + w, LEVS * channels, stride=ROWS), :] for i in range(4)] for w in range(2)
            ]
            left = jnp.concatenate([jnp.concatenate(side, axis=1) for side in sides], axis=0).astype(BF16)
            product = jnp.dot(left, tables[g, s, e], preferred_element_type=F32)
            tops = sum(sides[1][i] * last_rows[g, s, e, 0:1, i * 128 : i * 128 + 128] for i in range(4))
            if m > 0:
                product = totals[s, e] + product
                tops = last_totals[s, e] + tops
            if m < GROUPS - 1:
                totals[s, e] = product
                last_totals[s, e] = tops
            else:
                limit = (width - table[me * slot_count + s] - e + 1) // 2
                degree = lax.broadcasted_iota(jnp.int32, (LEVS * channels, product.shape[1]), 1)
                chosen = jnp.where(degree < limit, product[: LEVS * channels], product[LEVS * channels :])
                spectral[s, e, :, : degree_rows - 1] = chosen.astype(BF16)
                spectral[s, e, :, degree_rows - 1 :] = jnp.sum(tops, axis=1, keepdims=True).astype(BF16)
            return carry

        lax.fori_loop(0, 2 * slot_count, multiply, 0, unroll=2)

    sent = outgoing.at[pl.ds(0, DEVICES - 1)]
    pltpu.make_async_copy(sent, sent, send_sem).wait()


def on_device(fourier, table, legendre):
    lat_rows, channels, width = fourier.shape
    slot_count, _, degree_rows, half_lats = legendre.shape
    whole = degree_rows - 1
    return pl.pallas_call(
        fused,
        out_shape=jax.ShapeDtypeStruct((slot_count, 2, LEVS * channels, degree_rows), BF16),
        in_specs=[
            pl.BlockSpec(memory_space=pltpu.SMEM),
            pl.BlockSpec(memory_space=pltpu.HBM),
            pl.BlockSpec(memory_space=pltpu.HBM),
        ],
        out_specs=pl.BlockSpec(memory_space=pltpu.VMEM),
        scratch_shapes=[
            pltpu.VMEM((channels * lat_rows, width), BF16),
            pltpu.VMEM((RUN, ROWS, width), BF16),
            pltpu.VMEM((DEVICES, ROWS, channels * lat_rows), BF16),
            pltpu.VMEM((DEVICES, ROWS, channels * lat_rows), BF16),
            pltpu.VMEM((slot_count, degree_rows, 2, half_lats), BF16),
            pltpu.VMEM((GROUPS, slot_count, 2, 512, whole), BF16),
            pltpu.VMEM((256, 256), BF16),
            pltpu.VMEM((4, 256, 256), BF16),
            pltpu.VMEM((GROUPS, slot_count, 2, 8, 512), F32),
            pltpu.VMEM((4, 2, LEVS * channels * ROWS, 128), F32),
            pltpu.VMEM((slot_count, 2, 2 * LEVS * channels, whole), F32),
            pltpu.VMEM((slot_count, 2, LEVS * channels, 128), F32),
            pltpu.SemaphoreType.DMA((channels * lat_rows // 384,)),
            pltpu.SemaphoreType.DMA((slot_count,)),
            pltpu.SemaphoreType.DMA,
            pltpu.SemaphoreType.DMA((GROUPS,)),
            pltpu.SemaphoreType.DMA,
            pltpu.SemaphoreType.REGULAR,
        ],
        compiler_params=pltpu.CompilerParams(
            collective_id=0, has_side_effects=True, vmem_limit_bytes=63 << 20
        ),
    )(table, fourier.transpose(1, 0, 2), legendre.transpose(0, 2, 1, 3))


def solution(mesh):
    in_specs = (P("lat", "lev", None), P(), P(("lat", "lev"), None, None, None))
    out_specs = P(("lat", "lev"), None, None, None)
    return jax.shard_map(
        on_device, mesh=mesh, in_specs=in_specs, out_specs=out_specs, check_vma=False
    )
```

```python
import functools

import jax
import jax.numpy as jnp
from jax import lax
from jax.experimental import pallas as pl
from jax.experimental.pallas import tpu as pltpu
from jax.sharding import PartitionSpec as P

MESH = pl.DeviceIdType.MESH
F32, BF16 = jnp.float32, jnp.bfloat16
SIDE = 4
LEVS = 8
DEVICES = 128
GROUPS = 4
RUN = DEVICES // GROUPS
ROWS = 8
ORDER = (2 | 8 | 32, 32, 8, 16, 64)
NT = (((1,), (1,)), ((), ()))


def hop(i):
    bits = 0
    for place, mask in enumerate(ORDER):
        bits ^= (i >> place & 1) * mask
    return bits & 2, bits >> 2 & 2, bits >> 4 & 3, bits >> 6


def targets(m):
    lat, lev = lax.axis_index("lat"), lax.axis_index("lev")
    x, y, z, core = lat % SIDE + m % 2, lat // SIDE + m // 2, lev // 2, lev % 2
    xs = {d: (x + d) % SIDE for d in (0, 2)}
    ys = {d: (y + d) % SIDE * SIDE for d in (0, 2)}
    zs = {d: (z + d) % SIDE * 2 for d in range(SIDE)}
    lats = {(dx, dy): ys[dy] + xs[dx] for dx in xs for dy in ys}
    levs = {(dz, dc): zs[dz] + (core + dc) % 2 for dz in zs for dc in range(2)}
    hops = [hop(i) for i in range(RUN)]
    return [(lats[dx, dy], levs[dz, dc]) for dx, dy, dz, dc in hops]


def fused(
    table, fourier, legendre, spectral,
    rows_in, picks, outgoing, arrived, raw_tables, tables, spread, lanes, last_rows, parts, totals, last_totals,
    rows_sem, table_sem, send_sem, recv_sem, own_sem, all_sem,
):
    channels, lat_rows, width = fourier.shape
    slot_count, degree_rows = legendre.shape[0], legendre.shape[1]
    lat, lev = lax.axis_index("lat"), lax.axis_index("lev")
    x, y = lat % SIDE, lat // SIDE
    me = lat * LEVS + lev
    tail = lat_rows - 128
    fold = 128 // tail

    near = targets(0)[1:]
    links = [targets(m)[0] for m in range(1, GROUPS)]
    back = [((y - m // 2) % SIDE * SIDE + (x - m % 2) % SIDE, lev) for m in range(1, GROUPS)]
    barrier = pltpu.get_barrier_semaphore()
    for peer in near + links:
        pl.semaphore_signal(barrier, inc=1, device_id=peer, device_id_type=MESH)

    step = 384
    pieces = channels * lat_rows // step

    def piece(i):
        return rows_in.at[pl.ds(pl.multiple_of(i * step, 128), step)]

    for c in range(channels):
        pltpu.make_async_copy(
            fourier.at[c, pl.ds(0, 128)], rows_in.at[pl.ds(c * 128, 128)], rows_sem.at[c * 128 // step]
        ).start()
    for c in range(channels):
        pltpu.make_async_copy(
            fourier.at[c, pl.ds(128, tail)],
            rows_in.at[pl.ds(channels * 128 + c * tail, tail)],
            rows_sem.at[pieces - 1],
        ).start()
    for s in range(slot_count):
        pltpu.make_async_copy(legendre.at[s], raw_tables.at[s], table_sem.at[s]).start()

    sub = lax.broadcasted_iota(jnp.int32, (ROWS, 128), 0)
    lane = lax.broadcasted_iota(jnp.int32, (ROWS, 128), 1)

    def choose(m):
        for i, (to_lat, to_lev) in enumerate(targets(m)):
            first = (to_lat * LEVS + to_lev) * slot_count
            pair = jnp.full((ROWS, 128), table[first], jnp.int32)
            for s in range(1, slot_count):
                pair = jnp.where(sub // 2 == s, table[first + s], pair)
            column = jnp.where(sub % 2 == 0, pair, width - 1 - pair) - lane
            for t in range(width // 128):
                picks[i, :, t * 128 : t * 128 + 128] = jnp.where(column == t * 128, 1.0, 0.0).astype(BF16)

    def gather(m):
        choose(m)

        def some(i, carry):
            if m == 0:
                pltpu.make_async_copy(piece(i), piece(i), rows_sem.at[i]).wait()
            got = lax.dot_general(
                picks[...].reshape(RUN * ROWS, width), piece(i)[...], NT, preferred_element_type=F32
            )
            at = pl.ds(pl.multiple_of(i * step, 128), step)
            outgoing[m * RUN : (m + 1) * RUN, :, at] = got.astype(BF16).reshape(RUN, ROWS, step)
            return carry

        lax.fori_loop(0, pieces, some, 0)

    def send(m):
        for i, peer in enumerate(targets(m)):
            if m == 0 and i == 0:
                continue
            pltpu.make_async_remote_copy(
                src_ref=outgoing.at[m * RUN + i],
                dst_ref=arrived.at[me],
                send_sem=send_sem,
                recv_sem=recv_sem.at[m],
                device_id=peer,
                device_id_type=MESH,
            ).start()

    gather(0)
    pl.semaphore_wait(barrier, len(near) + len(links))
    for peer in back:
        pl.semaphore_signal(all_sem, inc=1, device_id=peer, device_id_type=MESH)
    send(0)
    own = pltpu.make_async_copy(outgoing.at[0], arrived.at[me], own_sem)
    own.start()
    gather(1)
    pl.semaphore_wait(all_sem, len(links))
    gather(2)
    send(1)
    gather(3)
    send(2)

    ri = lax.broadcasted_iota(jnp.int32, (256, 256), 0)
    ci = lax.broadcasted_iota(jnp.int32, (256, 256), 1)
    spread[...] = jnp.where(ci == ri % 128 * 2 + ri // 128, 1.0, 0.0).astype(BF16)
    source = jnp.where(ri < 128, ri, 128 + ri % tail)
    for q in range(fold):
        lanes[q] = jnp.where(ci == source + q * tail, 1.0, 0.0).astype(BF16)
    r_last = lax.broadcasted_iota(jnp.int32, (16, 256), 0)
    c_last = lax.broadcasted_iota(jnp.int32, (16, 256), 1)
    last = jnp.where(c_last == 254 + r_last // 8, 1.0, 0.0).astype(BF16)

    def relay(s, start, chooser):
        raw = raw_tables[s, pl.ds(start, 128)].reshape(256, raw_tables.shape[3])
        apart = jnp.dot(chooser, raw, preferred_element_type=F32).astype(BF16)
        for a in range(LEVS):
            low = lat_rows * a // 128 * 128
            yield a // SIDE * 2 + a % 2, a % SIDE // 2 * 256, apart[:, low : low + 256], lanes[a % fold]

    for s in range(slot_count):
        pltpu.make_async_copy(legendre.at[s], raw_tables.at[s], table_sem.at[s]).wait()

        def block(j, carry):
            at = pl.multiple_of(j * 128, 128)
            for g, place, apart, layout in relay(s, at, spread[...]):
                laid = lax.dot_general(layout, apart, NT, preferred_element_type=F32).astype(BF16)
                for e in range(2):
                    tables[g, s, e, place : place + 256, pl.ds(at, 128)] = laid[:, e * 128 : e * 128 + 128]
            return carry

        lax.fori_loop(0, degree_rows // 128, block, 0)
        for g, place, apart, layout in relay(s, degree_rows - 128, last):
            laid = lax.dot_general(apart, layout, NT, preferred_element_type=F32)
            for e in range(2):
                last_rows[g, s, e, :, place : place + 256] = laid[e * 8 : e * 8 + 8]
        if s == 0:
            send(3)

    own.wait()
    lane8 = lax.broadcasted_iota(jnp.int32, (ROWS, 128), 1)
    for m in range(GROUPS):
        count = DEVICES // GROUPS - (1 if m == 0 else 0)
        some = arrived.at[pl.ds(0, count)]
        pltpu.make_async_copy(some, some, recv_sem.at[m]).wait()
        from_x, from_y = (x + m) % 2, (y + m // 2) % 2
        g = from_y * 2 + from_x
        for half in range(2):
            north = from_y * SIDE + from_x + 2 * half

            def fold_in(b, carry):
                upper = arrived[north * LEVS + b].astype(F32)
                lower = arrived[(north + 8) * LEVS + b].astype(F32)
                for e, both in enumerate((upper + lower, upper - lower)):
                    for c in range(channels):
                        at = pl.ds(pl.multiple_of((b * channels + c) * ROWS, ROWS), ROWS)
                        parts[half * 2, e, at, :] = both[:, c * 128 : c * 128 + 128]
                        rest = channels * 128 + c // fold * 128
                        parts[half * 2 + 1, e, at, :] = jnp.where(
                            lane8 // tail == c % fold, both[:, rest : rest + 128], 0.0
                        )
                return carry

            lax.fori_loop(0, LEVS, fold_in, 0)

        def multiply(n, carry):
            s, e = n // 2, n % 2
            sides = [
                [parts[i, e, pl.ds(2 * s + w, LEVS * channels, stride=ROWS), :] for i in range(4)] for w in range(2)
            ]
            left = jnp.concatenate([jnp.concatenate(side, axis=1) for side in sides], axis=0).astype(BF16)
            product = jnp.dot(left, tables[g, s, e], preferred_element_type=F32)
            tops = sum(sides[1][i] * last_rows[g, s, e, 0:1, i * 128 : i * 128 + 128] for i in range(4))
            if m > 0:
                product = totals[s, e] + product
                tops = last_totals[s, e] + tops
            if m < GROUPS - 1:
                totals[s, e] = product
                last_totals[s, e] = tops
            else:
                limit = (width - table[me * slot_count + s] - e + 1) // 2
                degree = lax.broadcasted_iota(jnp.int32, (LEVS * channels, product.shape[1]), 1)
                chosen = jnp.where(degree < limit, product[: LEVS * channels], product[LEVS * channels :])
                spectral[s, e, :, : degree_rows - 1] = chosen.astype(BF16)
                spectral[s, e, :, degree_rows - 1 :] = jnp.sum(tops, axis=1, keepdims=True).astype(BF16)
            return carry

        lax.fori_loop(0, 2 * slot_count, multiply, 0, unroll=8 if m == GROUPS - 1 else 2)

    sent = outgoing.at[pl.ds(0, DEVICES - 1)]
    pltpu.make_async_copy(sent, sent, send_sem).wait()


def on_device(fourier, table, legendre):
    lat_rows, channels, width = fourier.shape
    slot_count, _, degree_rows, half_lats = legendre.shape
    whole = degree_rows - 1
    return pl.pallas_call(
        fused,
        out_shape=jax.ShapeDtypeStruct((slot_count, 2, LEVS * channels, degree_rows), BF16),
        in_specs=[
            pl.BlockSpec(memory_space=pltpu.SMEM),
            pl.BlockSpec(memory_space=pltpu.HBM),
            pl.BlockSpec(memory_space=pltpu.HBM),
        ],
        out_specs=pl.BlockSpec(memory_space=pltpu.VMEM),
        scratch_shapes=[
            pltpu.VMEM((channels * lat_rows, width), BF16),
            pltpu.VMEM((RUN, ROWS, width), BF16),
            pltpu.VMEM((DEVICES, ROWS, channels * lat_rows), BF16),
            pltpu.VMEM((DEVICES, ROWS, channels * lat_rows), BF16),
            pltpu.VMEM((slot_count, degree_rows, 2, half_lats), BF16),
            pltpu.VMEM((GROUPS, slot_count, 2, 512, whole), BF16),
            pltpu.VMEM((256, 256), BF16),
            pltpu.VMEM((4, 256, 256), BF16),
            pltpu.VMEM((GROUPS, slot_count, 2, 8, 512), F32),
            pltpu.VMEM((4, 2, LEVS * channels * ROWS, 128), F32),
            pltpu.VMEM((slot_count, 2, 2 * LEVS * channels, whole), F32),
            pltpu.VMEM((slot_count, 2, LEVS * channels, 128), F32),
            pltpu.SemaphoreType.DMA((channels * lat_rows // 384,)),
            pltpu.SemaphoreType.DMA((slot_count,)),
            pltpu.SemaphoreType.DMA,
            pltpu.SemaphoreType.DMA((GROUPS,)),
            pltpu.SemaphoreType.DMA,
            pltpu.SemaphoreType.REGULAR,
        ],
        compiler_params=pltpu.CompilerParams(
            collective_id=0, has_side_effects=True, vmem_limit_bytes=63 << 20
        ),
    )(table, fourier.transpose(1, 0, 2), legendre.transpose(0, 2, 1, 3))


def solution(mesh):
    in_specs = (P("lat", "lev", None), P(), P(("lat", "lev"), None, None, None))
    out_specs = P(("lat", "lev"), None, None, None)
    return jax.shard_map(
        on_device, mesh=mesh, in_specs=in_specs, out_specs=out_specs, check_vma=False
    )
```

```python
import functools

import jax
import jax.numpy as jnp
from jax import lax
from jax.experimental import pallas as pl
from jax.experimental.pallas import tpu as pltpu
from jax.sharding import PartitionSpec as P

MESH = pl.DeviceIdType.MESH
F32, BF16 = jnp.float32, jnp.bfloat16
SIDE = 4
LEVS = 8
DEVICES = 128
GROUPS = 4
RUN = DEVICES // GROUPS
ROWS = 8
ORDER = (2 | 8 | 32, 32, 8, 16, 64)
NT = (((1,), (1,)), ((), ()))


def hop(i):
    bits = 0
    for place, mask in enumerate(ORDER):
        bits ^= (i >> place & 1) * mask
    return bits & 2, bits >> 2 & 2, bits >> 4 & 3, bits >> 6


def targets(m):
    lat, lev = lax.axis_index("lat"), lax.axis_index("lev")
    x, y, z, core = lat % SIDE + m % 2, lat // SIDE + m // 2, lev // 2, lev % 2
    xs = {d: (x + d) % SIDE for d in (0, 2)}
    ys = {d: (y + d) % SIDE * SIDE for d in (0, 2)}
    zs = {d: (z + d) % SIDE * 2 for d in range(SIDE)}
    lats = {(dx, dy): ys[dy] + xs[dx] for dx in xs for dy in ys}
    levs = {(dz, dc): zs[dz] + (core + dc) % 2 for dz in zs for dc in range(2)}
    hops = [hop(i) for i in range(RUN)]
    return [(lats[dx, dy], levs[dz, dc]) for dx, dy, dz, dc in hops]


def fused(
    table, fourier, legendre, spectral,
    rows_in, picks, outgoing, arrived, raw_tables, tables, spread, lanes, last_rows, parts, totals, last_totals,
    rows_sem, table_sem, send_sem, recv_sem, own_sem, all_sem,
):
    channels, lat_rows, width = fourier.shape
    slot_count, degree_rows = legendre.shape[0], legendre.shape[1]
    lat, lev = lax.axis_index("lat"), lax.axis_index("lev")
    x, y = lat % SIDE, lat // SIDE
    me = lat * LEVS + lev
    tail = lat_rows - 128
    fold = 128 // tail

    near = targets(0)[1:]
    links = [targets(m)[0] for m in range(1, GROUPS)]
    back = [((y - m // 2) % SIDE * SIDE + (x - m % 2) % SIDE, lev) for m in range(1, GROUPS)]
    barrier = pltpu.get_barrier_semaphore()
    for peer in near + links:
        pl.semaphore_signal(barrier, inc=1, device_id=peer, device_id_type=MESH)

    step = 384
    pieces = channels * lat_rows // step

    def piece(i):
        return rows_in.at[pl.ds(pl.multiple_of(i * step, 128), step)]

    for c in range(channels):
        pltpu.make_async_copy(
            fourier.at[c, pl.ds(0, 128)], rows_in.at[pl.ds(c * 128, 128)], rows_sem.at[c * 128 // step]
        ).start()
    for c in range(channels):
        pltpu.make_async_copy(
            fourier.at[c, pl.ds(128, tail)],
            rows_in.at[pl.ds(channels * 128 + c * tail, tail)],
            rows_sem.at[pieces - 1],
        ).start()
    for s in range(slot_count):
        pltpu.make_async_copy(legendre.at[s], raw_tables.at[s], table_sem.at[s]).start()

    sub = lax.broadcasted_iota(jnp.int32, (ROWS, 128), 0)
    lane = lax.broadcasted_iota(jnp.int32, (ROWS, 128), 1)

    def choose(m):
        for i, (to_lat, to_lev) in enumerate(targets(m)):
            first = (to_lat * LEVS + to_lev) * slot_count
            pair = jnp.full((ROWS, 128), table[first], jnp.int32)
            for s in range(1, slot_count):
                pair = jnp.where(sub // 2 == s, table[first + s], pair)
            column = jnp.where(sub % 2 == 0, pair, width - 1 - pair) - lane
            for t in range(width // 128):
                picks[i, :, t * 128 : t * 128 + 128] = jnp.where(column == t * 128, 1.0, 0.0).astype(BF16)

    def gather(m):
        choose(m)

        def some(i, carry):
            if m == 0:
                pltpu.make_async_copy(piece(i), piece(i), rows_sem.at[i]).wait()
            got = lax.dot_general(
                picks[...].reshape(RUN * ROWS, width), piece(i)[...], NT, preferred_element_type=F32
            )
            at = pl.ds(pl.multiple_of(i * step, 128), step)
            outgoing[m * RUN : (m + 1) * RUN, :, at] = got.astype(BF16).reshape(RUN, ROWS, step)
            return carry

        lax.fori_loop(0, pieces, some, 0)

    def send(m):
        for i, peer in enumerate(targets(m)):
            if m == 0 and i == 0:
                continue
            pltpu.make_async_remote_copy(
                src_ref=outgoing.at[m * RUN + i],
                dst_ref=arrived.at[me],
                send_sem=send_sem,
                recv_sem=recv_sem.at[m],
                device_id=peer,
                device_id_type=MESH,
            ).start()

    gather(0)
    pl.semaphore_wait(barrier, len(near) + len(links))
    for peer in back:
        pl.semaphore_signal(all_sem, inc=1, device_id=peer, device_id_type=MESH)
    send(0)
    own = pltpu.make_async_copy(outgoing.at[0], arrived.at[me], own_sem)
    own.start()
    gather(1)
    pl.semaphore_wait(all_sem, len(links))
    gather(2)
    send(1)
    gather(3)
    send(2)

    ri = lax.broadcasted_iota(jnp.int32, (256, 256), 0)
    ci = lax.broadcasted_iota(jnp.int32, (256, 256), 1)
    spread[...] = jnp.where(ci == ri % 128 * 2 + ri // 128, 1.0, 0.0).astype(BF16)
    source = jnp.where(ri < 128, ri, 128 + ri % tail)
    for q in range(fold):
        lanes[q] = jnp.where(ci == source + q * tail, 1.0, 0.0).astype(BF16)
    r_last = lax.broadcasted_iota(jnp.int32, (16, 256), 0)
    c_last = lax.broadcasted_iota(jnp.int32, (16, 256), 1)
    last = jnp.where(c_last == 254 + r_last // 8, 1.0, 0.0).astype(BF16)

    def relay(s, start, chooser):
        raw = raw_tables[s, pl.ds(start, 128)].reshape(256, raw_tables.shape[3])
        apart = jnp.dot(chooser, raw, preferred_element_type=F32).astype(BF16)
        for a in range(LEVS):
            low = lat_rows * a // 128 * 128
            yield a // SIDE * 2 + a % 2, a % SIDE // 2 * 256, apart[:, low : low + 256], lanes[a % fold]

    for s in range(slot_count):
        pltpu.make_async_copy(legendre.at[s], raw_tables.at[s], table_sem.at[s]).wait()

        def block(j, carry):
            at = pl.multiple_of(j * 128, 128)
            for g, place, apart, layout in relay(s, at, spread[...]):
                laid = lax.dot_general(layout, apart, NT, preferred_element_type=F32).astype(BF16)
                for e in range(2):
                    tables[g, s, e, place : place + 256, pl.ds(at, 128)] = laid[:, e * 128 : e * 128 + 128]
            return carry

        lax.fori_loop(0, degree_rows // 128, block, 0)
        for g, place, apart, layout in relay(s, degree_rows - 128, last):
            laid = lax.dot_general(apart, layout, NT, preferred_element_type=F32)
            for e in range(2):
                last_rows[g, s, e, :, place : place + 256] = laid[e * 8 : e * 8 + 8]
        if s == 0:
            send(3)

    own.wait()
    lane8 = lax.broadcasted_iota(jnp.int32, (ROWS, 128), 1)
    for m in range(GROUPS):
        count = DEVICES // GROUPS - (1 if m == 0 else 0)
        some = arrived.at[pl.ds(0, count)]
        pltpu.make_async_copy(some, some, recv_sem.at[m]).wait()
        from_x, from_y = (x + m) % 2, (y + m // 2) % 2
        g = from_y * 2 + from_x
        for half in range(2):
            north = from_y * SIDE + from_x + 2 * half

            def fold_in(b, carry):
                upper = arrived[north * LEVS + b].astype(F32)
                lower = arrived[(north + 8) * LEVS + b].astype(F32)
                for e, both in enumerate((upper + lower, upper - lower)):
                    for c in range(channels):
                        at = pl.ds(pl.multiple_of((b * channels + c) * ROWS, ROWS), ROWS)
                        parts[half * 2, e, at, :] = both[:, c * 128 : c * 128 + 128]
                        rest = channels * 128 + c // fold * 128
                        parts[half * 2 + 1, e, at, :] = jnp.where(
                            lane8 // tail == c % fold, both[:, rest : rest + 128], 0.0
                        )
                return carry

            lax.fori_loop(0, LEVS, fold_in, 0)

        def multiply(n, carry):
            s, e = n // 2, n % 2
            sides = [
                [parts[i, e, pl.ds(2 * s + w, LEVS * channels, stride=ROWS), :] for i in range(4)] for w in range(2)
            ]
            left = jnp.concatenate([jnp.concatenate(side, axis=1) for side in sides], axis=0).astype(BF16)
            product = jnp.dot(left, tables[g, s, e], preferred_element_type=F32)
            tops = sum(sides[1][i] * last_rows[g, s, e, 0:1, i * 128 : i * 128 + 128] for i in range(4))
            if m > 0:
                product = totals[s, e] + product
                tops = last_totals[s, e] + tops
            if m < GROUPS - 1:
                totals[s, e] = product
                last_totals[s, e] = tops
            else:
                limit = (width - table[me * slot_count + s] - e + 1) // 2
                degree = lax.broadcasted_iota(jnp.int32, (LEVS * channels, product.shape[1]), 1)
                chosen = jnp.where(degree < limit, product[: LEVS * channels], product[LEVS * channels :])
                spectral[s, e, :, : degree_rows - 1] = chosen.astype(BF16)
                spectral[s, e, :, degree_rows - 1 :] = jnp.sum(tops, axis=1, keepdims=True).astype(BF16)
            return carry

        lax.fori_loop(0, 2 * slot_count, multiply, 0, unroll=8 if m >= GROUPS - 2 else 2)

    sent = outgoing.at[pl.ds(0, DEVICES - 1)]
    pltpu.make_async_copy(sent, sent, send_sem).wait()


def on_device(fourier, table, legendre):
    lat_rows, channels, width = fourier.shape
    slot_count, _, degree_rows, half_lats = legendre.shape
    whole = degree_rows - 1
    return pl.pallas_call(
        fused,
        out_shape=jax.ShapeDtypeStruct((slot_count, 2, LEVS * channels, degree_rows), BF16),
        in_specs=[
            pl.BlockSpec(memory_space=pltpu.SMEM),
            pl.BlockSpec(memory_space=pltpu.HBM),
            pl.BlockSpec(memory_space=pltpu.HBM),
        ],
        out_specs=pl.BlockSpec(memory_space=pltpu.VMEM),
        scratch_shapes=[
            pltpu.VMEM((channels * lat_rows, width), BF16),
            pltpu.VMEM((RUN, ROWS, width), BF16),
            pltpu.VMEM((DEVICES, ROWS, channels * lat_rows), BF16),
            pltpu.VMEM((DEVICES, ROWS, channels * lat_rows), BF16),
            pltpu.VMEM((slot_count, degree_rows, 2, half_lats), BF16),
            pltpu.VMEM((GROUPS, slot_count, 2, 512, whole), BF16),
            pltpu.VMEM((256, 256), BF16),
            pltpu.VMEM((4, 256, 256), BF16),
            pltpu.VMEM((GROUPS, slot_count, 2, 8, 512), F32),
            pltpu.VMEM((4, 2, LEVS * channels * ROWS, 128), F32),
            pltpu.VMEM((slot_count, 2, 2 * LEVS * channels, whole), F32),
            pltpu.VMEM((slot_count, 2, LEVS * channels, 128), F32),
            pltpu.SemaphoreType.DMA((channels * lat_rows // 384,)),
            pltpu.SemaphoreType.DMA((slot_count,)),
            pltpu.SemaphoreType.DMA,
            pltpu.SemaphoreType.DMA((GROUPS,)),
            pltpu.SemaphoreType.DMA,
            pltpu.SemaphoreType.REGULAR,
        ],
        compiler_params=pltpu.CompilerParams(
            collective_id=0, has_side_effects=True, vmem_limit_bytes=63 << 20
        ),
    )(table, fourier.transpose(1, 0, 2), legendre.transpose(0, 2, 1, 3))


def solution(mesh):
    in_specs = (P("lat", "lev", None), P(), P(("lat", "lev"), None, None, None))
    out_specs = P(("lat", "lev"), None, None, None)
    return jax.shard_map(
        on_device, mesh=mesh, in_specs=in_specs, out_specs=out_specs, check_vma=False
    )
```
